32 devices in a mesh: ctx: 8 (over y, x, core), fsdp: 4 (over z).
Axes of the slice: x: 2, y: 2, z: 4, core: 2. Of those that a mesh axis runs over, the one named last changes fastest.
Arguments:
- tokens: bfloat16 [4, 2048, 768], P('fsdp', 'ctx'), may hold values from -6 to 6
- segments: int32 [4, 2048], P('fsdp'), may hold values from 0 to 15, never falling along the last dimension, each value on 1 to 1536 neighbouring positions
- w_query: bfloat16 [768, 768], P('fsdp'), may hold values from -0.3125 to 0.3125
- b_query: bfloat16 [768], P('fsdp'), may hold values from -3 to 3
- w_key: bfloat16 [768, 768], P('fsdp'), may hold values from -0.3125 to 0.3125
- w_value: bfloat16 [768, 768], P('fsdp'), may hold values from -0.21875 to 0.21875
- b_value: bfloat16 [768], P('fsdp'), may hold values from -3 to 3
- w_out: bfloat16 [768, 768], P('fsdp'), may hold values from -1.75 to 1.75
- b_out: bfloat16 [768], P('fsdp'), may hold values from -3 to 3
- gain_attention: bfloat16 [768], P('fsdp'), may hold values from 0.099609375 to 1.8984375
- bias_attention: bfloat16 [768], P('fsdp'), may hold values from -3 to 3
- w_inner: bfloat16 [768, 3072], P('fsdp'), may hold values from -0.21875 to 0.21875
- b_inner: bfloat16 [3072], P('fsdp'), may hold values from -3 to 3
- w_outer: bfloat16 [3072, 768], P('fsdp'), may hold values from -0.109375 to 0.109375
- b_outer: bfloat16 [768], P('fsdp'), may hold values from -3 to 3
- gain_feed: bfloat16 [768], P('fsdp'), may hold values from 0.099609375 to 1.8984375
- bias_feed: bfloat16 [768], P('fsdp'), may hold values from -3 to 3
- cotangent: bfloat16 [4, 2048, 768], P('fsdp', 'ctx'), may hold values from -6 to 6
Outputs:
- output: bfloat16 [4, 2048, 768], P('fsdp', 'ctx')
- grad_input: float32 [4, 2048, 768], P('fsdp', 'ctx')
- grad_w_query: float32 [768, 768], P('fsdp')
- grad_b_query: float32 [768], P('fsdp')
- grad_w_key: float32 [768, 768], P('fsdp')
- grad_w_value: float32 [768, 768], P('fsdp')
- grad_b_value: float32 [768], P('fsdp')
- grad_w_out: float32 [768, 768], P('fsdp')
- grad_b_out: float32 [768], P('fsdp')
- grad_gain_attention: float32 [768], P('fsdp')
- grad_bias_attention: float32 [768], P('fsdp')
- grad_w_inner: float32 [768, 3072], P('fsdp')
- grad_b_inner: float32 [3072], P('fsdp')
- grad_w_outer: float32 [3072, 768], P('fsdp')
- grad_b_outer: float32 [768], P('fsdp')
- grad_gain_feed: float32 [768], P('fsdp')
- grad_bias_feed: float32 [768], P('fsdp')
The draws below stay inside these ranges and needn't reach their ends.
Inputs may be any that keep to these rules, and one draw needn't show every extreme that they name: `segments`: along a sequence the document numbers never fall; each document has 1 to 1536 tokens, and one has exactly 1536.
All inputs are finite; a program needn't handle non-finite values.
Results may differ from the reference program's by a relative error of at most 0.023.
Values may be sent and summed in bfloat16 or wider, within the bound.
No kernel may reach another device: no remote copies, remote signals or barrier semaphores. Data moves between devices by JAX's collectives and lax.ppermute only.
A program may use at most 128 MiB of HBM per device.

```python
import math
import jax
import jax.numpy as jnp
import numpy as np
from jax import lax

D = 768
HEADS = 12
FF = 3072
DOCS = 16
LENGTH = 2048
LONGEST = 1536
SEQS = 4


def steps_of(key, shape, shards, low, top_value):
    def one(position, blocks):
        steps = jax.random.uniform(jax.random.fold_in(jax.random.fold_in(key, 6), position), (blocks,), jnp.float32, low / len(shards), top_value / len(shards))
        return jnp.repeat(jnp.exp(steps), shape[position] // blocks).reshape((-1,) + (1,) * (len(shape) - position - 1))

    factor_of = one(*shards[0])
    for cut in shards[1:]:
        factor_of = factor_of * one(*cut)
    return factor_of


def length_profile(count, total, most, lean):
    portions = [(1 << 20) // math.isqrt(rank ** lean) + 1 for rank in range(2, count + 1)]
    surplus, given = total - most - (count - 1), [1] * (count - 1)
    while surplus > 0:
        free = [i for i in range(count - 1) if given[i] < most]
        whole, budget = sum([portions[i] for i in free]), surplus
        for i in free:
            extra = min(most - given[i], max(1, budget * portions[i] // whole), surplus)
            given[i] = given[i] + extra
            surplus = surplus - extra
    return np.array([most] + given)


def uneven_parts(own_key, number_of, total, reach, skew):
    if number_of == 2:
        one = jax.random.randint(own_key, (), max(1, total - reach), min(reach, total - 1) + 1)
        return jnp.stack([one, total - one])
    tallies = jnp.asarray(length_profile(number_of, total, reach, skew), jnp.int32)
    couples = (number_of - 1) // 2
    donor, sink = tallies[1:1 + 2 * couples:2], tallies[2:2 + 2 * couples:2]
    slack = jnp.minimum(donor - 1, reach - sink)
    shifted = jax.random.randint(jax.random.fold_in(own_key, 1), (couples,), 0, 1 << 20) % (slack + 1)
    tallies = tallies.at[1:1 + 2 * couples:2].set(donor - shifted).at[2:2 + 2 * couples:2].set(sink + shifted)
    return tallies[jax.random.permutation(jax.random.fold_in(own_key, 2), number_of)]


def gaussian(key, shape, deviation, most, shards=(), dtype=jnp.bfloat16):
    entries = deviation * jax.random.normal(key, shape, jnp.float32)
    if shards:
        entries = entries * steps_of(key, shape, shards, -0.22, 0.18)
    return jnp.clip(entries, -most, most).astype(dtype)


def setup_inputs(seed: int = 0) -> dict:
    streams_of = jax.random.split(jax.random.key(seed), 19)
    tokens = gaussian(streams_of[0], (SEQS, LENGTH, D), 1.0, 6.0, ((0, 4), (1, 8)))
    segments = jax.vmap(lambda own: jnp.searchsorted(jnp.cumsum(uneven_parts(own, DOCS, LENGTH, LONGEST, 2)), jnp.arange(LENGTH), side="right"))(jax.random.split(streams_of[1], SEQS)).reshape((SEQS, LENGTH)).astype(jnp.int32)
    w_query = gaussian(streams_of[2], (D, D), (D // 2) ** -0.5, 0.3125, ((0, 4),))
    b_query = gaussian(streams_of[3], (D,), 0.5, 3.0, ((0, 4),))
    w_key = gaussian(streams_of[4], (D, D), (D // 2) ** -0.5, 0.3125, ((0, 4),))
    w_value = gaussian(streams_of[5], (D, D), D ** -0.5, 0.21875, ((0, 4),))
    b_value = gaussian(streams_of[6], (D,), 0.5, 3.0, ((0, 4),))
    w_out = gaussian(streams_of[7], (D, D), (D // 64) ** -0.5, 1.75, ((0, 4),))
    b_out = gaussian(streams_of[8], (D,), 0.5, 3.0, ((0, 4),))
    gain_attention = jnp.clip(1.0 + 0.18 * jax.random.normal(streams_of[9], (D,), jnp.float32), 0.099609375, 1.8984375).astype(jnp.bfloat16)
    bias_attention = gaussian(streams_of[10], (D,), 0.5, 3.0, ((0, 4),))
    w_inner = gaussian(streams_of[11], (D, FF), D ** -0.5, 0.21875, ((0, 4),))
    b_inner = gaussian(streams_of[12], (FF,), 0.5, 3.0, ((0, 4),))
    w_outer = gaussian(streams_of[13], (FF, D), FF ** -0.5, 0.109375, ((0, 4),))
    b_outer = gaussian(streams_of[14], (D,), 0.5, 3.0, ((0, 4),))
    gain_feed = jnp.clip(1.0 + 0.18 * jax.random.normal(streams_of[15], (D,), jnp.float32), 0.099609375, 1.8984375).astype(jnp.bfloat16)
    bias_feed = gaussian(streams_of[16], (D,), 0.5, 3.0, ((0, 4),))
    cotangent = gaussian(streams_of[17], (SEQS, LENGTH, D), 1.0, 6.0, ((0, 4), (1, 8)))
    return dict(tokens=tokens, segments=segments, w_query=w_query, b_query=b_query, w_key=w_key, w_value=w_value, b_value=b_value, w_out=w_out, b_out=b_out, gain_attention=gain_attention, bias_attention=bias_attention, w_inner=w_inner, b_inner=b_inner, w_outer=w_outer, b_outer=b_outer, gain_feed=gain_feed, bias_feed=bias_feed, cotangent=cotangent)


@jax.custom_vjp
def low(v):
    return lax.optimization_barrier(v.astype(jnp.bfloat16)).astype(jnp.float32)

@jax.custom_vjp
def low_back(v):
    return v

def low_keep(v):
    return (low(v), None)

def low_pass(kept, grad):
    return (grad,)

def back_keep(v):
    return (v, None)

def back_low(kept, grad):
    return (low(grad),)
low.defvjp(low_keep, low_pass)
low_back.defvjp(back_keep, back_low)
ln_epsilon = 1e-12
highest = lax.Precision.HIGHEST

def layer_norm(values, gain, bias):
    center = values - lax.optimization_barrier(jnp.mean(values, axis=-1, keepdims=True))
    spread = lax.optimization_barrier(jnp.mean(center * center, axis=-1, keepdims=True))
    return center * lax.rsqrt(spread + ln_epsilon) * gain + bias

def product(left, right):
    return jnp.dot(left, right, precision=highest, preferred_element_type=jnp.float32)

def round_both(values):
    return low(low_back(values))

def layer_one(params, inputs, seg_all):
    w_query, b_query, w_key, w_value, b_value, w_out, b_out, gain_attention, bias_attention, w_inner, b_inner, w_outer, b_outer, gain_feed, bias_feed = params
    length = inputs.shape[0]
    head_size = inputs.shape[1] // HEADS
    block = math.gcd(length, 512)
    query = round_both(product(inputs, w_query) + b_query)
    keys = round_both(product(inputs, w_key)).reshape(length, HEADS, head_size)
    values = round_both(product(inputs, w_value) + b_value).reshape(length, HEADS, head_size)
    query_blocks = query.reshape(length // block, block, HEADS, head_size)
    seg_blocks = seg_all.reshape(length // block, block)

    def attend(pair):
        rows_query, seg_query = pair
        scores = jnp.einsum('bhd,lhd->hbl', rows_query, keys, precision=highest) * 0.125
        allowed = (seg_query[:, None] == seg_all[None, :])[None]
        scores = low_back(jnp.where(allowed, scores, -1e+30))
        total = jax.nn.logsumexp(scores, axis=-1, keepdims=True)
        weights = low(jnp.exp(scores - total))
        mixed = jnp.einsum('hbl,lhd->bhd', weights, values, precision=highest)
        return mixed.reshape(block, HEADS * head_size)
    attended = lax.map(jax.checkpoint(attend), (query_blocks, seg_blocks)).reshape(length, HEADS * head_size)
    attended = round_both(attended)
    branch = low_back(product(attended, w_out) + b_out)
    normed = layer_norm(inputs + branch, gain_attention, bias_attention)
    inner = low_back(product(low(normed), w_inner) + b_inner)
    active = low(jax.nn.gelu(inner, approximate=False))
    outer = low_back(product(active, w_outer) + b_outer)
    return layer_norm(normed + outer, gain_feed, bias_feed)

def reference(tokens, segments, w_query, b_query, w_key, w_value, b_value, w_out, b_out, gain_attention, bias_attention, w_inner, b_inner, w_outer, b_outer, gain_feed, bias_feed, cotangent):
    params = (w_query.astype(jnp.float32), b_query.astype(jnp.float32), w_key.astype(jnp.float32), w_value.astype(jnp.float32), b_value.astype(jnp.float32), w_out.astype(jnp.float32), b_out.astype(jnp.float32), gain_attention.astype(jnp.float32), bias_attention.astype(jnp.float32), w_inner.astype(jnp.float32), b_inner.astype(jnp.float32), w_outer.astype(jnp.float32), b_outer.astype(jnp.float32), gain_feed.astype(jnp.float32), bias_feed.astype(jnp.float32))
    inputs = tokens.astype(jnp.float32)

    def forward(weights, layer_in):

        def single(pair):
            return layer_one(weights, pair[0], pair[1])
        return lax.map(single, (layer_in, segments))
    result, pull = jax.vjp(forward, params, inputs)
    grads, grad_input = pull(cotangent.astype(jnp.float32))
    return (result.astype(jnp.bfloat16), grad_input, grads[0], grads[1], grads[2], grads[3], grads[4], grads[5], grads[6], grads[7], grads[8], grads[9], grads[10], grads[11], grads[12], grads[13], grads[14])
```

```python
import functools
import math

import jax
import jax.numpy as jnp
from jax import lax
from jax.experimental import pallas as pl
from jax.experimental.pallas import tpu as pltpu
from jax.sharding import PartitionSpec as P

HEADS = 12
GROUPS = 4
LN_EPS = 1e-12
MASKED = -1e30
f32 = jnp.float32
b16 = jnp.bfloat16


def swap(x, axis, flip):
    return lax.ppermute(x, axis, [(i, i ^ flip) for i in range(lax.axis_size(axis))])


def pick(x, index):
    return lax.dynamic_index_in_dim(x, index, 0, keepdims=False)


def nn(a, b):
    return lax.dot_general(a, b, (((1,), (0,)), ((), ())), preferred_element_type=f32)


def nt(a, b):
    return lax.dot_general(a, b, (((1,), (1,)), ((), ())), preferred_element_type=f32)


def tn(a, b):
    return lax.dot_general(a, b, (((0,), (0,)), ((), ())), preferred_element_type=f32)


def whole_call(body, outs, n_in, scratch=(), name=None):
    specs = [pl.BlockSpec(memory_space=pltpu.SMEM)]
    specs += [pl.BlockSpec(memory_space=pltpu.VMEM)] * (n_in - 1)
    return pl.pallas_call(
        body,
        out_shape=outs,
        in_specs=specs,
        out_specs=[pl.BlockSpec(memory_space=pltpu.VMEM)] * len(outs),
        scratch_shapes=list(scratch),
        name=name,
    )


def shape(dims, dtype):
    return jax.ShapeDtypeStruct(dims, dtype)


def row_sum(x):
    return jnp.sum(x, axis=0, keepdims=True)


def normalised(x):
    center = x - jnp.mean(x, axis=-1, keepdims=True)
    spread = jnp.mean(center * center, axis=-1, keepdims=True)
    rate = lax.rsqrt(spread + LN_EPS)
    return center * rate, rate


def norm_back(u, hat, rate):
    along = jnp.mean(u * hat, axis=-1, keepdims=True)
    return rate * (u - jnp.mean(u, axis=-1, keepdims=True) - hat * along)


def project_kernel(sc, t0, t1, t2, t3, own, par, shift, q_out, kv_out, w_out):
    z, c = sc[0], sc[1]
    ranks, half = own.shape[0], own.shape[1]
    width = q_out.shape[-1]
    for a in range(ranks):
        base = (z ^ a) * (2 * half)
        w_out[pl.ds(pl.multiple_of(base + c * half, 16), half), :] = own[a]
        w_out[pl.ds(pl.multiple_of(base + (1 - c) * half, 16), half), :] = par[a]
    for s, t in enumerate((t0, t1, t2, t3)):
        y = nn(t[...], w_out[...]) + shift[...]
        q_out[s] = y[:, :width].astype(b16)
        kv_out[s] = y[:, width:].astype(b16)


def project_back_kernel(sc, t0, t1, t2, t3, dq, dkv, dkv_in, w, dx_own, dx_send, gw, gb):
    width = dq.shape[-1]
    grads = []
    for s in range(GROUPS):
        right = (dkv[s] + dkv_in[s].astype(f32)).astype(b16)
        grads.append(jnp.concatenate([dq[s], right], axis=1))
    dx_own[...] = nt(grads[0], w[...])
    for s in range(1, GROUPS):
        dx_send[s - 1] = nt(grads[s], w[...]).astype(b16)
    total = tn(t0[...], grads[0])
    sums = row_sum(grads[0].astype(f32))
    for s, t in ((1, t1), (2, t2), (3, t3)):
        total += tn(t[...], grads[s])
        sums += row_sum(grads[s].astype(f32))
    gw[...] = total.astype(b16)
    gb[...] = sums


def block_of(sc, entry, s):
    rank = sc[2] ^ entry
    return ((rank >> 1) * GROUPS + (sc[3] ^ s)) * 2 + (rank & 1)


def gather_blocks(sc, parts, kv_all):
    @pl.when(pl.program_id(0) == 0)
    def _():
        for entry, part in enumerate(parts):
            for s in range(GROUPS):
                kv_all[block_of(sc, entry, s)] = part[s]


def attend_kernel(sc, span, q, seg_rows, seg_cols, *rest):
    parts, (mixed, low_out, log_out), (kv_all, kept) = rest[:-5], rest[-5:-2], rest[-2:]
    gather_blocks(sc, parts, kv_all)
    here = block_of(sc, 0, pl.program_id(0))
    low, high = span[here, 0], span[here, 1]
    rows = q.shape[1]
    per_group = q.shape[2] // 128
    seg_q = seg_rows[here]
    left = lax.broadcasted_iota(jnp.int32, (rows, 128), 1) < 64
    one = jnp.ones((rows, 128), b16)
    log_out[...] = jnp.zeros(log_out.shape, f32)
    for h in range(per_group):
        lanes = slice(h * 128, (h + 1) * 128)
        qh = q[0, :, lanes]

        def first(j, top, lanes=lanes, qh=qh):
            st = nt(kv_all[j, :, lanes], qh)
            seg = seg_cols[j]
            for w in range(0, rows, 128):
                ok = seg == seg_q[:, w : w + 128]
                kept[j, :, w : w + 128] = jnp.where(ok, st[:, w : w + 128], MASKED)
            return jnp.maximum(top, jnp.max(kept[j], axis=0, keepdims=True))

        top = lax.fori_loop(low, high, first, jnp.full((1, rows), MASKED, f32))

        def second(j, state, lanes=lanes, top=top):
            total, acc = state
            pt = jnp.exp(kept[j] - top)
            values = jnp.where(left, one, kv_all[j, :, lanes])
            return total + row_sum(pt), acc + tn(pt.astype(b16), values)

        total, acc = lax.fori_loop(
            low, high, second, (jnp.zeros((1, rows), f32), jnp.zeros((rows, 128), f32))
        )
        out = acc[:, 64:] / acc[:, :64]
        mixed[0, :, h * 64 : (h + 1) * 64] = out
        low_out[0, :, h * 64 : (h + 1) * 64] = out.astype(b16)
        log_out[0, h : h + 1, :] = top + jnp.log(total)


def attend_back_kernel(sc, span, q, seg_rows, seg_cols, grad, mixed, logs, *rest):
    count = (len(rest) - 4) // 2
    parts = rest[:count]
    dq, dkv_own = rest[count], rest[count + 1]
    dkv_send = rest[count + 2 : 2 * count + 1]
    kv_all, dkv_all, dq_acc = rest[2 * count + 1 :]
    step = pl.program_id(0)
    gather_blocks(sc, parts, kv_all)

    @pl.when(step == 0)
    def _():
        dkv_all[...] = jnp.zeros(dkv_all.shape, f32)

    here = block_of(sc, 0, step)
    low, high = span[here, 0], span[here, 1]
    rows = q.shape[1]
    per_group = q.shape[2] // 128
    seg_q = seg_rows[here]
    gap = jnp.zeros((rows, 64), b16)
    for h in range(per_group):
        lanes = slice(h * 128, (h + 1) * 128)
        part = slice(h * 64, (h + 1) * 64)
        qh = q[0, :, lanes]
        gh = grad[0, :, part]
        along = jnp.sum(gh.astype(f32) * mixed[0, :, part], axis=1, keepdims=True)
        balance = jnp.transpose(jnp.broadcast_to(along, (rows, 128)))[0:1]
        gh = jnp.concatenate([gap, gh], axis=1)
        log_row = logs[0, h : h + 1, :]
        dq_acc[...] = jnp.zeros(dq_acc.shape, f32)
        both = jnp.concatenate([qh, gh], axis=0)

        @pl.loop(low, high)
        def _(j, lanes=lanes, qh=qh, gh=gh, balance=balance, log_row=log_row, both=both):
            kv = kv_all[j, :, lanes]
            seg = seg_cols[j]
            ok = jnp.concatenate([seg == seg_q[:, w : w + 128] for w in range(0, rows, 128)], axis=1)
            st = jnp.where(ok, nt(kv, qh), MASKED)
            pt = jnp.exp(st - log_row)
            dst = (pt * (nt(kv, gh) - balance)).astype(b16)
            dkv_all[j, :, lanes] += nn(jnp.concatenate([dst, pt.astype(b16)], axis=1), both)
            dq_acc[...] += tn(dst, kv)

        keep = lax.broadcasted_iota(jnp.int32, (rows, 128), 1) < 64
        dq[0, :, lanes] = jnp.where(keep, dq_acc[...], 0.0).astype(b16)

    @pl.when(step == pl.num_programs(0) - 1)
    def _():
        for s in range(GROUPS):
            dkv_own[s] = dkv_all[block_of(sc, 0, s)]
            for entry, send in enumerate(dkv_send):
                send[s] = dkv_all[block_of(sc, entry + 1, s)].astype(b16)


def lay_out(sc, pieces, own, par):
    z, c = sc[0], sc[1]
    ranks, rows = own.shape[0], own.shape[1]
    for a in range(ranks):
        at = pl.ds(pl.multiple_of((z ^ a) * rows, 16), rows)
        pieces[c, at, :] = own[a]
        pieces[1 - c, at, :] = par[a]


def group_rows(sc, s, size):
    return pl.ds(pl.multiple_of((sc[3] ^ s) * size, 16), size)


def out_kernel(sc, tok, a0, a1, a2, a3, own, par, shift, gain, bias, hat, rate, low, w):
    lay_out(sc, w, own, par)
    size = a0.shape[1]
    half = w.shape[2]
    sides = []
    for side in range(2):
        y = tok[:, side * half : (side + 1) * half].astype(f32)
        for s, a in enumerate((a0, a1, a2, a3)):
            y += nn(a[...], w[side, group_rows(sc, s, size), :])
        sides.append(y)
    resid = jnp.concatenate(sides, axis=1) + shift[...]
    h, r = normalised(resid)
    hat[...] = h
    rate[...] = jnp.broadcast_to(r, rate.shape)
    low[...] = (h * gain[...] + bias[...]).astype(b16)


def weights_of(sc, pieces, w):
    z = sc[0]
    rows = pieces.shape[1]
    for a in range(pieces.shape[0]):
        w[pl.ds(pl.multiple_of((z ^ a) * rows, 16), rows), :] = pieces[a]


def feed_kernel(sc, n_own, n_par, i0, i1, i2, i3, o0, o1, o2, o3, shift, act, slope, y_own, y_par, wi, wo):
    rows = n_own.shape[0]
    tokens = jnp.concatenate([n_own[...], n_par[...]], axis=0)
    total = jnp.zeros((2 * rows, n_own.shape[1]), f32)
    for s, (i, o) in enumerate(((i0, o0), (i1, o1), (i2, o2), (i3, o3))):
        weights_of(sc, i, wi.at[s])
        weights_of(sc, o, wo.at[s])
        inner = nn(tokens, wi[s]) + shift[s : s + 1, :]
        phi = 0.5 * (1.0 + lax.erf(inner * math.sqrt(0.5)))
        dens = jnp.exp(-0.5 * inner * inner) * (1.0 / math.sqrt(2.0 * math.pi))
        a = (inner * phi).astype(b16)
        act[s] = a
        slope[s] = (phi + inner * dens).astype(slope.dtype)
        total += nn(a, wo[s])
    y_own[...] = total[:rows]
    y_par[...] = total[rows:]


def close_kernel(sc, hat1, gain1, bias1, y_own, y_par, shift, gain, bias, cot, result, grad_two, low, sums):
    normed = hat1[...] * gain1[...] + bias1[...]
    h, r = normalised(normed + y_own[...] + y_par[...] + shift[...])
    result[...] = (h * gain[...] + bias[...]).astype(b16)
    c = cot[...].astype(f32)
    g = norm_back(c * gain[...], h, r)
    grad_two[...] = g
    g_low = g.astype(b16)
    low[...] = g_low
    sums[...] = jnp.zeros(sums.shape, f32)
    sums[0:1, :] = row_sum(g_low.astype(f32))
    sums[1:2, :] = row_sum(c * h)
    sums[2:3, :] = row_sum(c)


def feed_back_kernel(sc, g_own, g_par, i0, i1, i2, i3, o0, o1, o2, o3, slope, gi_out, y_own, y_par, gb, wi, wo):
    rows = g_own.shape[0]
    grads = jnp.concatenate([g_own[...], g_par[...]], axis=0)
    total = jnp.zeros((2 * rows, g_own.shape[1]), f32)
    for s, (i, o) in enumerate(((i0, o0), (i1, o1), (i2, o2), (i3, o3))):
        weights_of(sc, i, wi.at[s])
        weights_of(sc, o, wo.at[s])
        gi = (nt(grads, wo[s]) * slope[s].astype(f32)).astype(b16)
        gi_out[s] = gi
        gb[s : s + 1, :] = row_sum(gi.astype(f32))
        total += nt(gi, wi[s])
    y_own[...] = total[:rows]
    y_par[...] = total[rows:]


def feed_weights_kernel(sc, n_own, n_par, g_own, g_par, act, gi, wi0, wi1, wi2, wi3, wo0, wo1, wo2, wo3):
    tokens = jnp.concatenate([n_own[...], n_par[...]], axis=0)
    grads = jnp.concatenate([g_own[...], g_par[...]], axis=0)
    for s, (i, o) in enumerate(((wi0, wo0), (wi1, wo1), (wi2, wo2), (wi3, wo3))):
        i[...] = tn(tokens, gi[s]).astype(b16)
        o[...] = tn(act[s], grads).astype(b16)


def first_back_kernel(sc, grad_two, y_own, y_par, hat, rate, gain, own, par, a0, a1, a2, a3,
                      grad_one, b0, b1, b2, b3, gw_own, gw_par, sums, w):
    lay_out(sc, w, own, par)
    c = sc[1]
    gn = grad_two[...] + y_own[...] + y_par[...]
    h = hat[...]
    g = norm_back(gn * gain[...], h, rate[:, 0:1])
    grad_one[...] = g
    g_low = g.astype(b16)
    sums[...] = jnp.zeros(sums.shape, f32)
    sums[0:1, :] = row_sum(g_low.astype(f32))
    sums[1:2, :] = row_sum(gn * h)
    sums[2:3, :] = row_sum(gn)
    half = w.shape[2]
    lo, hi = g_low[:, :half], g_low[:, half:]
    mine = jnp.where(c == 0, lo, hi)
    other = jnp.where(c == 0, hi, lo)
    for s, (a, b) in enumerate(((a0, b0), (a1, b1), (a2, b2), (a3, b3))):
        at = group_rows(sc, s, b.shape[1])
        b[...] = (nt(lo, w[0, at, :]) + nt(hi, w[1, at, :])).astype(b16)
        gw_own[at, :] = tn(a[...], mine)
        gw_par[at, :] = tn(a[...], other).astype(b16)


def per_device(
    tokens,
    segments,
    w_query,
    b_query,
    w_key,
    w_value,
    b_value,
    w_out,
    b_out,
    gain_attention,
    bias_attention,
    w_inner,
    b_inner,
    w_outer,
    b_outer,
    gain_feed,
    bias_feed,
    cotangent,
):
    n = lax.axis_size("ctx")
    ranks = lax.axis_size("fsdp")
    place = lax.axis_index("ctx")
    z = lax.axis_index("fsdp")
    rows, d = tokens.shape[1], tokens.shape[2]
    ff = w_inner.shape[1]
    c, chip = place & 1, place >> 1
    g, r = chip % GROUPS, chip // GROUPS
    sets = n // GROUPS
    rank = r * 2 + c
    per_group = HEADS // GROUPS
    hd = d // HEADS
    gw = per_group * hd
    dz, fz = d // ranks, ff // ranks
    half = dz // 2
    piece = fz // (2 * GROUPS)
    wide = per_group * 2 * hd
    sc = jnp.stack([z, c, rank, g]).astype(jnp.int32)

    def over_z(x):
        return [x] + [swap(x, "fsdp", a) for a in range(1, ranks)]

    def over_group(x):
        return [x] + [swap(x, "ctx", s << 1) for s in range(1, GROUPS)]

    def over_sets(x):
        flips = [(t & 1) | ((t >> 1) * 2 * GROUPS) for t in range(sets)]
        return [x if f == 0 else swap(x, "ctx", f) for f in flips]

    tok = tokens[0]
    toks = over_group(tok)

    def head_columns(w):
        return lax.dynamic_slice_in_dim(w, g * gw, gw, 1).reshape(dz, per_group, hd)

    wq = head_columns(w_query) * jnp.asarray(0.125, b16)
    packed = jnp.concatenate(
        [
            jnp.concatenate([wq, jnp.zeros_like(wq)], axis=2).reshape(dz, wide),
            jnp.concatenate([head_columns(w_key), head_columns(w_value)], axis=2).reshape(dz, wide),
        ],
        axis=1,
    )
    vectors = jnp.concatenate(
        [b_query, b_value, b_out, gain_attention, bias_attention, b_outer, gain_feed, bias_feed, b_inner]
    )
    nvec = vectors.shape[0]
    vrows = -(-nvec // d)
    extra = -(-vrows // 8) * 8
    vec_rows = jnp.pad(vectors, (0, extra * d - nvec)).reshape(extra, d)
    first = jnp.concatenate([lax.dynamic_slice_in_dim(packed, c * half, half, 0), vec_rows], axis=0)
    first_all = jnp.stack(over_z(first))
    proj_own = first_all[:, :half]
    proj_par = swap(proj_own, "ctx", 1)
    order = z ^ jnp.arange(ranks)
    vec_all = jnp.take(first_all[:, half:].reshape(ranks, extra * d), order, axis=0)[:, :nvec].astype(f32)
    vec = [vec_all[:, k * dz : (k + 1) * dz].reshape(1, d) for k in range(8)]
    v_query, v_value, v_out, v_gain1, v_bias1, v_outer, v_gain2, v_bias2 = vec
    v_inner = vec_all[:, 8 * dz :].reshape(ranks, 2 * GROUPS, piece)

    own_piece = c * GROUPS + g
    wi = lax.dynamic_slice_in_dim(w_inner.reshape(dz, ranks, fz), own_piece * piece, piece, 2)
    wi_z = jnp.stack(over_z(wi.reshape(dz, ranks * piece)))
    wo_z = jnp.stack(over_z(lax.dynamic_slice_in_dim(w_outer, own_piece * piece, piece, 0)))
    wout_own = jnp.stack(over_z(lax.dynamic_slice_in_dim(w_out, c * (d // 2), d // 2, 1)))
    wout_par = swap(wout_own, "ctx", 1)
    wi1, wi2 = swap(wi_z, "ctx", 2), swap(wi_z, "ctx", 4)
    wi3 = swap(wi1, "ctx", 4)
    wo1, wo2 = swap(wo_z, "ctx", 2), swap(wo_z, "ctx", 4)
    wo3 = swap(wo2, "ctx", 2)
    wis, wos = (wi_z, wi1, wi2, wi3), (wo_z, wo1, wo2, wo3)
    group_order = g ^ jnp.arange(GROUPS)
    shift_inner = jnp.take(
        v_inner.transpose(1, 0, 2).reshape(2 * GROUPS, ranks * piece), c * GROUPS + group_order, axis=0
    )

    def of_group(v):
        return pick(v.reshape(GROUPS, per_group, hd), g)

    bq = of_group(v_query) * 0.125
    bv = of_group(v_value)
    zero = jnp.zeros_like(bq)
    shift_qkv = jnp.concatenate(
        [jnp.concatenate([bq, zero], axis=1).reshape(1, wide), jnp.concatenate([zero, bv], axis=1).reshape(1, wide)],
        axis=1,
    )
    q, kv, w_qkv = whole_call(
        project_kernel,
        [shape((GROUPS, rows, wide), b16), shape((GROUPS, rows, wide), b16), shape((d, 2 * wide), b16)],
        8,
        name="project",
    )(sc, *toks, proj_own, proj_par, shift_qkv)
    kvs = over_sets(kv)

    seg = segments[0].reshape(n, rows)
    begin, end = seg[:, 0], seg[:, -1]
    span = jnp.stack(
        [
            jnp.sum((end[None, :] < begin[:, None]).astype(jnp.int32), axis=1),
            jnp.sum((begin[None, :] <= end[:, None]).astype(jnp.int32), axis=1),
        ],
        axis=1,
    )
    seg_rows = seg.reshape(n, 1, rows)
    seg_cols = jnp.broadcast_to(seg[:, :, None], (n, rows, 128))

    smem = pl.BlockSpec(memory_space=pltpu.SMEM)

    def fixed(dims):
        return pl.BlockSpec(dims, lambda s: (0,) * len(dims))

    def stepped(dims):
        return pl.BlockSpec((1,) + dims, lambda s: (s,) + (0,) * len(dims))

    kv_specs = [fixed((GROUPS, rows, wide))] * sets
    mixed, att_low, logs = pl.pallas_call(
        attend_kernel,
        grid=(GROUPS,),
        in_specs=[smem, smem, stepped((rows, wide)), fixed((n, 1, rows)), fixed((n, rows, 128))] + kv_specs,
        out_specs=[stepped((rows, gw)), stepped((rows, gw)), stepped((8, rows))],
        out_shape=[
            shape((GROUPS, rows, gw), f32),
            shape((GROUPS, rows, gw), b16),
            shape((GROUPS, 8, rows), f32),
        ],
        scratch_shapes=[pltpu.VMEM((n, rows, wide), b16), pltpu.VMEM((n, rows, rows), f32)],
        name="attend",
    )(sc, span, q, seg_rows, seg_cols, *kvs)

    atts = [att_low[0]] + [swap(att_low[s], "ctx", s << 1) for s in range(1, GROUPS)]

    hat1, rate1, low = whole_call(
        out_kernel,
        [shape((rows, d), f32), shape((rows, 128), f32), shape((rows, d), b16)],
        11,
        [pltpu.VMEM((2, d, d // 2), b16)],
        name="out",
    )(sc, tok, *atts, wout_own, wout_par, v_out, v_gain1, v_bias1)
    low_par = swap(low, "ctx", 1)

    cols = ranks * piece
    scratch = [pltpu.VMEM((GROUPS, d, cols), b16), pltpu.VMEM((GROUPS, cols, d), b16)]
    act, slope, y_own, y_send = whole_call(
        feed_kernel,
        [
            shape((GROUPS, 2 * rows, cols), b16),
            shape((GROUPS, 2 * rows, cols), b16),
            shape((rows, d), f32),
            shape((rows, d), f32),
        ],
        12,
        scratch,
        name="feed",
    )(sc, low, low_par, *wis, *wos, shift_inner)
    y_par = swap(y_send, "ctx", 1)

    result, grad_two, gol, sums_two = whole_call(
        close_kernel,
        [shape((rows, d), b16), shape((rows, d), f32), shape((rows, d), b16), shape((8, d), f32)],
        10,
        name="close",
    )(sc, hat1, v_gain1, v_bias1, y_own, y_par, v_outer, v_gain2, v_bias2, cotangent[0])
    gol_par = swap(gol, "ctx", 1)

    gi, gn_own, gn_send, gb_inner = whole_call(
        feed_back_kernel,
        [
            shape((GROUPS, 2 * rows, cols), b16),
            shape((rows, d), f32),
            shape((rows, d), f32),
            shape((GROUPS, cols), f32),
        ],
        12,
        scratch,
        name="feed_back",
    )(sc, gol, gol_par, *wis, *wos, slope)
    gn_par = swap(gn_send, "ctx", 1)

    gws = whole_call(
        feed_weights_kernel,
        [shape((d, cols), b16)] * GROUPS + [shape((cols, d), b16)] * GROUPS,
        7,
        name="feed_weights",
    )(sc, low, low_par, gol, gol_par, act, gi)
    gwi, gwo = gws[:GROUPS], gws[GROUPS:]

    grad_one, *ga, gwout_own, gwout_send, sums_one = whole_call(
        first_back_kernel,
        [shape((rows, d), f32)]
        + [shape((rows, gw), b16)] * GROUPS
        + [shape((d, d // 2), f32), shape((d, d // 2), b16), shape((8, d), f32)],
        13,
        [pltpu.VMEM((2, d, d // 2), b16)],
        name="first_back",
    )(sc, grad_two, gn_own, gn_par, hat1, rate1, v_gain1, wout_own, wout_par, *atts)

    grads_att = jnp.stack([ga[0]] + [swap(ga[s], "ctx", s << 1) for s in range(1, GROUPS)])

    dq, dkv_own, *dkv_send = pl.pallas_call(
        attend_back_kernel,
        grid=(GROUPS,),
        in_specs=[smem, smem, stepped((rows, wide)), fixed((n, 1, rows)), fixed((n, rows, 128))]
        + [stepped((rows, gw)), stepped((rows, gw)), stepped((8, rows))]
        + kv_specs,
        out_specs=[stepped((rows, wide)), fixed((GROUPS, rows, wide))] + kv_specs[1:],
        out_shape=[shape((GROUPS, rows, wide), b16), shape((GROUPS, rows, wide), f32)]
        + [shape((GROUPS, rows, wide), b16)] * (sets - 1),
        scratch_shapes=[
            pltpu.VMEM((n, rows, wide), b16),
            pltpu.VMEM((n, rows, wide), f32),
            pltpu.VMEM((rows, 128), f32),
        ],
        name="attend_back",
    )(sc, span, q, seg_rows, seg_cols, grads_att, mixed, logs, *kvs)
    flips = [(t & 1) | ((t >> 1) * 2 * GROUPS) for t in range(sets)]
    dkv_in = swap(dkv_send[0], "ctx", flips[1])
    for t in range(2, sets):
        dkv_own = dkv_own + swap(dkv_send[t - 1], "ctx", flips[t]).astype(f32)

    dx_own, dx_send, gw_qkv, gb_qkv = whole_call(
        project_back_kernel,
        [
            shape((rows, d), f32),
            shape((GROUPS - 1, rows, d), b16),
            shape((d, 2 * wide), b16),
            shape((1, 2 * wide), f32),
        ],
        9,
        name="project_back",
    )(sc, *toks, dq, dkv_own, dkv_in, w_qkv)
    grad_input = grad_one + dx_own
    for s in range(1, GROUPS):
        grad_input = grad_input + swap(dx_send[s - 1], "ctx", s << 1).astype(f32)

    wi_in, wo_in = swap(gwi[3], "ctx", 2), swap(gwo[3], "ctx", 4)
    gwi2 = (gwi[2].astype(f32) + wi_in.astype(f32)).astype(b16)
    gwo1 = (gwo[1].astype(f32) + wo_in.astype(f32)).astype(b16)

    def added(first, *others):
        total = first.astype(f32)
        for other in others:
            total = total + other.astype(f32)
        return total

    swi = added(gwi[0], swap(gwi[1], "ctx", 2), swap(gwi2, "ctx", 4))
    swo = added(gwo[0], swap(gwo1, "ctx", 2), swap(gwo[2], "ctx", 4))

    def over_r(x):
        total = x
        for t in range(1, sets // 2):
            total = total + swap(x.astype(b16), "ctx", t * 2 * GROUPS).astype(f32)
        return total

    def scatter_z(x):
        low_x = x.astype(b16)
        total = pick(x, z)
        for a in range(1, ranks):
            total = total + swap(pick(low_x, z ^ a), "fsdp", a).astype(f32)
        return total.astype(b16)

    fwi = scatter_z(over_r(swi).reshape(ranks, dz, cols))
    fwo = scatter_z(over_r(swo).reshape(ranks, piece, d))
    gwout = gwout_own + swap(gwout_send, "ctx", 1).astype(f32)
    fwout = scatter_z(gwout.reshape(ranks, dz, d // 2))

    gq, gkv = gb_qkv[0, :wide].reshape(per_group, 2, hd), gb_qkv[0, wide:].reshape(per_group, 2, hd)
    mine = (jnp.arange(GROUPS) == g).astype(f32)[:, None]
    gb_query = (mine * (gq[:, 0] * 0.125).reshape(1, gw)).reshape(d)
    gb_value = (mine * gkv[:, 1].reshape(1, gw)).reshape(d)
    gbi = jnp.take(gb_inner, group_order, axis=0).reshape(GROUPS, ranks, piece).transpose(1, 0, 2)
    gbi = gbi.reshape(ranks, 1, GROUPS * piece) * (jnp.arange(2) == c).astype(f32)[None, :, None]
    vec_grads = [gb_query, gb_value, sums_one[0], sums_one[1], sums_one[2], sums_two[0], sums_two[1], sums_two[2]]
    vec_parts = jnp.concatenate([v.reshape(ranks, dz) for v in vec_grads] + [gbi.reshape(ranks, fz)], axis=1)
    vec_parts = jnp.pad(vec_parts, ((0, 0), (0, extra * d - nvec))).reshape(ranks, extra, d)

    gw4 = gw_qkv.reshape(ranks, 2, half, 2 * wide)
    keep = lax.dynamic_index_in_dim(gw4, c, 1, keepdims=False)
    give = lax.dynamic_index_in_dim(gw4, 1 - c, 1, keepdims=False)
    gqkv = over_r(keep.astype(f32) + swap(give, "ctx", 1).astype(f32))
    fqkv = scatter_z(jnp.concatenate([gqkv, vec_parts], axis=1))

    def everywhere(x):
        pieces = jnp.stack(over_group(x))
        return jnp.stack([pieces, swap(pieces, "ctx", 1)])

    all_wi, all_wo, all_wout, all_qkv = everywhere(fwi), everywhere(fwo), everywhere(fwout), everywhere(fqkv)
    core_order = c ^ jnp.arange(2)

    def ordered(x):
        return jnp.take(jnp.take(x, core_order, axis=0), group_order, axis=1)

    d_inner = ordered(all_wi).reshape(2 * GROUPS, dz, ranks, piece).transpose(1, 2, 0, 3).reshape(dz, ff)
    d_outer = ordered(all_wo).reshape(fz, d)
    d_out = jnp.take(jnp.sum(all_wout.astype(f32), axis=1), core_order, axis=0)
    d_out = d_out.transpose(1, 0, 2).reshape(dz, d)
    qkv = ordered(all_qkv[:, :, :half])
    qkv = qkv.transpose(0, 2, 1, 3).reshape(dz, GROUPS, 2, per_group, 2, hd).astype(f32)
    d_query = qkv[:, :, 0, :, 0].reshape(dz, d) * 0.125
    d_key = qkv[:, :, 1, :, 0].reshape(dz, d)
    d_value = qkv[:, :, 1, :, 1].reshape(dz, d)
    v_here = jnp.sum(all_qkv[:, :, half:].astype(f32), axis=(0, 1))
    v, d_out_here = v_here, d_out
    for t in range(1, sets // 2):
        v = v + swap(v_here, "ctx", t * 2 * GROUPS)
        d_out = d_out + swap(d_out_here, "ctx", t * 2 * GROUPS)
    v = v.reshape(-1)
    vs = [v[k * dz : (k + 1) * dz] for k in range(8)]

    return (
        result[None],
        grad_input[None],
        d_query,
        vs[0],
        d_key,
        d_value.astype(f32),
        vs[1],
        d_out,
        vs[2],
        vs[3],
        vs[4],
        d_inner.astype(f32),
        v[8 * dz : 8 * dz + fz],
        d_outer.astype(f32),
        vs[5],
        vs[6],
        vs[7],
    )


def solution(mesh):
    rows = P("fsdp", "ctx", None)
    matrix = P("fsdp", None)
    vector = P("fsdp")
    return jax.shard_map(
        per_device,
        mesh=mesh,
        in_specs=(rows, matrix, matrix, vector, matrix, matrix, vector, matrix, vector, vector, vector)
        + (matrix, vector, matrix, vector, vector, vector, rows),
        out_specs=(rows, rows, matrix, vector, matrix, matrix, vector, matrix, vector, vector, vector)
        + (matrix, vector, matrix, vector, vector, vector),
        check_vma=False,
    )
```

```python
import functools
import math

import jax
import jax.numpy as jnp
from jax import lax
from jax.experimental import pallas as pl
from jax.experimental.pallas import tpu as pltpu
from jax.sharding import PartitionSpec as P

HEADS = 12
GROUPS = 4
LN_EPS = 1e-12
MASKED = -1e30
f32 = jnp.float32
b16 = jnp.bfloat16


def swap(x, axis, flip):
    return lax.ppermute(x, axis, [(i, i ^ flip) for i in range(lax.axis_size(axis))])


def after(x, *others):
    return lax.optimization_barrier((x,) + others)[0]


def nn(a, b):
    return lax.dot_general(a, b, (((1,), (0,)), ((), ())), preferred_element_type=f32)


def nt(a, b):
    return lax.dot_general(a, b, (((1,), (1,)), ((), ())), preferred_element_type=f32)


def tn(a, b):
    return lax.dot_general(a, b, (((0,), (0,)), ((), ())), preferred_element_type=f32)


COSTS = dict(
    pack_first=2, pack_feed=3, split_second=1, vectors=2, project=5, attend=11, out=4, feed=8, close=4, feed_back=8, feed_weights_far=4, first_back=4,
    out_weights=3, feed_weights=7, attend_back=22, project_weights=6, spread=3, spread_feed=3, spread_out=2, project_back=4,
    finish=3, finish_feed=5,
)


def cost(name):
    return pl.CostEstimate(flops=COSTS[name] * 10**10, bytes_accessed=10**6, transcendentals=0)


def whole_call(body, outs, n_in, scratch=(), name=None):
    specs = [pl.BlockSpec(memory_space=pltpu.SMEM)]
    specs += [pl.BlockSpec(memory_space=pltpu.VMEM)] * (n_in - 1)
    return pl.pallas_call(
        body,
        out_shape=outs,
        in_specs=specs,
        out_specs=[pl.BlockSpec(memory_space=pltpu.VMEM)] * len(outs),
        scratch_shapes=list(scratch),
        name=name,
        cost_estimate=cost(name),
    )


def shape(dims, dtype):
    return jax.ShapeDtypeStruct(dims, dtype)


def row_sum(x):
    return jnp.sum(x, axis=0, keepdims=True)


def normalised(x):
    center = x - jnp.mean(x, axis=-1, keepdims=True)
    spread = jnp.mean(center * center, axis=-1, keepdims=True)
    rate = lax.rsqrt(spread + LN_EPS)
    return center * rate, rate


def norm_back(u, hat, rate):
    along = jnp.mean(u * hat, axis=-1, keepdims=True)
    return rate * (u - jnp.mean(u, axis=-1, keepdims=True) - hat * along)


def pack_first_kernel(sc, wq, wk, wv, v0, v1, v2, v3, v4, v5, v6, v7, v8, out):
    c, g = sc[1], sc[3]
    half = wq.shape[0] // 2
    d = out.shape[1]
    gw, hd = d // GROUPS, d // HEADS
    at = pl.ds(pl.multiple_of(c * half, 16), half)
    gap = jnp.zeros((half, hd), b16)
    for k in range(GROUPS):

        @pl.when(g == k)
        def _(k=k):
            parts = []
            for h in range(gw // hd):
                lanes = slice(k * gw + h * hd, k * gw + (h + 1) * hd)
                parts += [wq[at, lanes] * jnp.asarray(0.125, b16), gap]
            for h in range(gw // hd):
                lanes = slice(k * gw + h * hd, k * gw + (h + 1) * hd)
                parts += [wk[at, lanes], wv[at, lanes]]
            out[:half] = jnp.concatenate(parts, axis=1)

    dz = v0.shape[0]
    each = d // dz
    cells = [v[...].reshape(1, -1) for v in (v0, v1, v2, v3, v4, v5, v6, v7, v8)]
    cells.append(jnp.zeros((1, d - v8.shape[0] % d), b16))
    lines, line, used = [], [], 0
    for cell in cells:
        line.append(cell)
        used += cell.shape[1]
        if used == d:
            lines.append(jnp.concatenate(line, axis=1))
            line, used = [], 0
    lines.append(jnp.zeros((8 - len(lines), d), b16))
    out[half:] = jnp.concatenate(lines, axis=0)


def pack_feed_kernel(sc, w_in, w_outer, w_out, inner, second):
    c, g = sc[1], sc[3]
    piece = second.shape[0] - w_out.shape[0] // 2
    ranks = inner.shape[1] // piece
    span = 2 * GROUPS * piece
    half, width = w_out.shape[0] // 2, w_out.shape[1] // 2
    own = c * GROUPS + g
    for k in range(2 * GROUPS):

        @pl.when(own == k)
        def _(k=k):
            lanes = [slice(y * span + k * piece, y * span + (k + 1) * piece) for y in range(ranks)]
            inner[...] = jnp.concatenate([w_in[:, at] for at in lanes], axis=1)

    second[:piece] = w_outer[pl.ds(pl.multiple_of(own * piece, 16), piece), :]
    for core in range(2):

        @pl.when(c == core)
        def _(core=core):
            for side in range(2):
                part = w_out[side * half : (side + 1) * half, core * width : (core + 1) * width]
                second[piece:, side * width : (side + 1) * width] = part


def split_second_kernel(sc, *refs):
    outer, out = refs[-2:]
    piece = outer.shape[1]
    for a, part in enumerate(refs[:-2]):
        outer[a] = part[:piece]
        out[a] = part[piece:]


def project_kernel(sc, t0, t1, t2, t3, own, par, shift, q_out, kv_out, w_out):
    z, c = sc[0], sc[1]
    ranks, half = own.shape[0], own.shape[1]
    width = q_out.shape[-1]
    for a in range(ranks):
        base = (z ^ a) * (2 * half)
        w_out[pl.ds(pl.multiple_of(base + c * half, 16), half), :] = own[a]
        w_out[pl.ds(pl.multiple_of(base + (1 - c) * half, 16), half), :] = par[a]
    for s, t in enumerate((t0, t1, t2, t3)):
        y = nn(t[...], w_out[...]) + shift[...]
        q_out[s] = y[:, :width].astype(b16)
        kv_out[s] = y[:, width:].astype(b16)


def project_weights_kernel(sc, t0, t1, t2, t3, dq_far, dq_near, dkv, dkv_in, sums_one, sums_two, keep, give, sums, both, total):
    ranks, half = keep.shape[0], give.shape[1]
    c = sc[1]
    width = dq_far.shape[-1]
    dqs = (dq_near[1], dq_near[0], dq_far[1], dq_far[0])
    column = jnp.zeros((1, 2 * width), f32)
    for s, t in enumerate((t0, t1, t2, t3)):
        both[s, :, :width] = dqs[s]
        both[s, :, width:] = (dkv[s] + dkv_in[s].astype(f32)).astype(b16)
        column += row_sum(both[s].astype(f32))
    total[...] = nn(jnp.concatenate([t0[...], t1[...], t2[...], t3[...]], axis=0).T, both[...].reshape(-1, 2 * width))
    for a in range(ranks):
        base = a * 2 * half
        keep[a] = total[pl.ds(pl.multiple_of(base + c * half, 16), half), :]
        give[a] = total[pl.ds(pl.multiple_of(base + (1 - c) * half, 16), half), :].astype(b16)
    sums[...] = jnp.concatenate([column, sums_one[0:3], sums_two[0:3], jnp.zeros((1, 2 * width), f32)], axis=0)


def project_back_kernel(sc, both, w, grad_one, dx_own, dx1, dx2, dx3):
    dx_own[...] = grad_one[...] + nt(both[0], w[...])
    for s, out in ((1, dx1), (2, dx2), (3, dx3)):
        out[...] = nt(both[s], w[...]).astype(b16)


def spread_kernel(sc, keep, got, sums, own, *sends):
    z = sc[0]
    half = got.shape[1]
    own[:half] = keep[z] + got[z].astype(f32)
    own[half:] = sums[...]
    for a, send in enumerate(sends):
        send[:half] = (keep[z ^ (a + 1)] + got[z ^ (a + 1)].astype(f32)).astype(b16)
        send[half:] = sums[...].astype(b16)


def spread_feed_kernel(sc, mine, left, right, own, *sends):
    z = sc[0]
    for a, out in enumerate((own,) + sends):
        k = z ^ a
        out[...] = (mine[k].astype(f32) + left[k].astype(f32) + right[k].astype(f32)).astype(out.dtype)


def spread_out_kernel(sc, mine, other, own, *sends):
    z = sc[0]
    for a, out in enumerate((own,) + sends):
        out[...] = (mine[z ^ a].astype(f32) + other[z ^ a].astype(f32)).astype(out.dtype)


def vectors_kernel(sc, rows, outs, shift_qkv, shift_inner, full, inner):
    z, c, g = sc[0], sc[1], sc[3]
    ranks = rows.shape[0]
    d = full.shape[1]
    dz = d // ranks
    piece = inner.shape[1] // ranks
    for k in range(ranks):
        row = rows[z ^ k].astype(f32)
        each = d // dz
        for j in range(8):
            low = (j % each) * dz
            full[j : j + 1, k * dz : (k + 1) * dz] = row[j // each : j // each + 1, low : low + dz]
        last = row[8 // each : 8 // each + 1]
        for j in range(2 * GROUPS):
            inner[j : j + 1, k * piece : (k + 1) * piece] = last[:, j * piece : (j + 1) * piece]
    outs[...] = full[...]
    gw = d // GROUPS
    hd = d // HEADS
    query, value = jnp.zeros((1, gw), f32), jnp.zeros((1, gw), f32)
    for k in range(GROUPS):
        query = jnp.where(g == k, full[0:1, k * gw : (k + 1) * gw], query)
        value = jnp.where(g == k, full[1:2, k * gw : (k + 1) * gw], value)
    gap = jnp.zeros((1, hd), f32)
    parts = []
    for h in range(gw // hd):
        parts += [query[:, h * hd : (h + 1) * hd] * 0.125, gap]
    for h in range(gw // hd):
        parts += [gap, value[:, h * hd : (h + 1) * hd]]
    shift_qkv[...] = jnp.concatenate(parts, axis=1)
    for s in range(GROUPS):
        shift_inner[s : s + 1, :] = inner[pl.ds(c * GROUPS + (g ^ s), 1), :]


def block_of(sc, entry, s):
    rank = sc[2] ^ entry
    return ((rank >> 1) * GROUPS + (sc[3] ^ s)) * 2 + (rank & 1)


def gather_blocks(sc, parts, kv_all):
    @pl.when(pl.program_id(0) == 0)
    def _():
        for entry, part in enumerate(parts):
            for s in range(GROUPS):
                kv_all[block_of(sc, entry, s)] = part[s]


def attend_kernel(start, sc, span, q, seg_rows, seg_cols, *rest):
    parts, (mixed, low_out, log_out), (kv_all, kept, top, acc) = rest[:-7], rest[-7:-4], rest[-4:]
    gather_blocks(sc, parts, kv_all)
    here = block_of(sc, 0, start - pl.program_id(0))
    low, high = span[here, 0], span[here, 1]
    rows = q.shape[1]
    per_group = q.shape[2] // 128
    left = lax.broadcasted_iota(jnp.int32, (rows, 128), 1) < 64
    one = jnp.ones((rows, 128), b16)
    seg_q = seg_cols[here]
    for h in range(per_group):
        top[h] = jnp.full((rows, 128), MASKED, f32)
        acc[h] = jnp.zeros((rows, 128), f32)

    @pl.loop(low, high)
    def _(j):
        seg = seg_rows[j]
        for h in range(per_group):
            lanes = slice(h * 128, (h + 1) * 128)
            s = nt(q[0, :, lanes], kv_all[j, :, lanes])
            best = top[h]
            for w in range(0, rows, 128):
                part = jnp.where(seg_q == seg[:, w : w + 128], s[:, w : w + 128], MASKED)
                kept[h, j, :, w : w + 128] = part
                best = jnp.maximum(best, part)
            top[h] = best

    for h in range(per_group):
        top[h] = jnp.broadcast_to(jnp.max(top[h], axis=1, keepdims=True), (rows, 128))

    @pl.loop(low, high)
    def _(j):
        for h in range(per_group):
            lanes = slice(h * 128, (h + 1) * 128)
            m = top[h]
            p = jnp.concatenate([jnp.exp(kept[h, j, :, w : w + 128] - m).astype(b16) for w in range(0, rows, 128)], axis=1)
            acc[h] += nn(p, jnp.where(left, one, kv_all[j, :, lanes]))

    log_out[...] = jnp.zeros(log_out.shape, f32)
    for h in range(per_group):
        a = acc[h]
        out = a[:, 64:] / a[:, :64]
        mixed[0, :, h * 64 : (h + 1) * 64] = out
        low_out[0, :, h * 64 : (h + 1) * 64] = out.astype(b16)
        log = top[h] + jnp.log(jnp.broadcast_to(a[:, 0:1], (rows, 128)))
        log_out[0, h : h + 1, :] = jnp.transpose(log)[0:1]


def attend_back_kernel(start, sc, span, q, seg_rows, seg_cols, *rest):
    count, begins, ends = start[1], start[2], start[3]
    grads, rest = rest[:count], rest[count:]
    mixed, logs = rest[:2]
    spare = len(rest) - (7 if begins else 8)
    sets = spare // 2 if ends else spare - 1
    parts, rest = rest[2 : 2 + sets], rest[2 + sets :]
    if not begins:
        before, rest = rest[0], rest[1:]
    dq, dkv_out, dkv_send = rest[0], rest[1], rest[2:-4]
    kv_all, dkv_all, dq_acc, both = rest[-4:]
    step = pl.program_id(0)
    gather_blocks(sc, parts, kv_all)

    @pl.when(step == 0)
    def _():
        dkv_all[...] = jnp.zeros(dkv_all.shape, f32) if begins else before[...]

    here = block_of(sc, 0, start[0] - step)
    low, high = span[here, 0], span[here, 1]
    rows = q.shape[1]
    per_group = q.shape[2] // 128
    seg_q = seg_rows[here]
    gap = jnp.zeros((rows, 64), b16)
    grad = grads[0][...]
    for k in range(1, count):
        grad = jnp.where(step == k, grads[k][...], grad)
    balance = []
    for h in range(per_group):
        part = slice(h * 64, (h + 1) * 64)
        gh = grad[:, part]
        along = jnp.sum(gh.astype(f32) * mixed[0, :, part], axis=1, keepdims=True)
        balance.append(jnp.transpose(jnp.broadcast_to(along, (rows, 128)))[0:1])
        both[h, :rows] = q[0, :, h * 128 : (h + 1) * 128]
        both[h, rows:] = jnp.concatenate([gap, gh], axis=1)
        dq_acc[h] = jnp.zeros((rows, 128), f32)

    @pl.loop(low, high)
    def _(j):
        seg = seg_cols[j]
        ok = jnp.concatenate([seg == seg_q[:, w : w + 128] for w in range(0, rows, 128)], axis=1)
        for h in range(per_group):
            lanes = slice(h * 128, (h + 1) * 128)
            kv = kv_all[j, :, lanes]
            pair = nt(kv, both[h])
            pt = jnp.exp(jnp.where(ok, pair[:, :rows], MASKED) - logs[0, h : h + 1, :])
            dst = (pt * (pair[:, rows:] - balance[h])).astype(b16)
            dkv_all[j, :, lanes] += nn(jnp.concatenate([dst, pt.astype(b16)], axis=1), both[h])
            dq_acc[h] += tn(dst, kv)

    keep = lax.broadcasted_iota(jnp.int32, (rows, 128), 1) < 64
    for h in range(per_group):
        dq[0, :, h * 128 : (h + 1) * 128] = jnp.where(keep, dq_acc[h], 0.0).astype(b16)

    @pl.when(step == pl.num_programs(0) - 1)
    def _():
        if not ends:
            dkv_out[...] = dkv_all[...]
        else:
            for s in range(GROUPS):
                dkv_out[s] = dkv_all[block_of(sc, 0, s)]
                for entry, send in enumerate(dkv_send):
                    send[s] = dkv_all[block_of(sc, entry + 1, s)].astype(b16)


def lay_out(sc, pieces, own, par):
    z, c = sc[0], sc[1]
    ranks, half, width = own.shape[0], own.shape[1], own.shape[2] // 2
    for a in range(ranks):
        for side in range(2):
            at = pl.ds(pl.multiple_of((z ^ a) * 2 * half + side * half, 16), half)
            pieces[c, at, :] = own[a, :, side * width : (side + 1) * width]
            pieces[1 - c, at, :] = par[a, :, side * width : (side + 1) * width]


def group_rows(sc, s, size):
    return pl.ds(pl.multiple_of((sc[3] ^ s) * size, 16), size)


def out_kernel(sc, tok, a0, a1, a2, a3, own, par, vec, hat, rate, low, w):
    lay_out(sc, w, own, par)
    size = a0.shape[1]
    half = w.shape[2]
    sides = []
    for side in range(2):
        y = tok[:, side * half : (side + 1) * half].astype(f32)
        for s, a in enumerate((a0, a1, a2, a3)):
            y += nn(a[...], w[side, group_rows(sc, s, size), :])
        sides.append(y)
    resid = jnp.concatenate(sides, axis=1) + vec[2:3]
    h, r = normalised(resid)
    hat[...] = h
    rate[...] = jnp.broadcast_to(r, rate.shape)
    low[...] = (h * vec[3:4] + vec[4:5]).astype(b16)


def weights_of(sc, pieces, w):
    z = sc[0]
    rows = pieces.shape[1]
    for a in range(pieces.shape[0]):
        w[pl.ds(pl.multiple_of((z ^ a) * rows, 16), rows), :] = pieces[a]


def feed_kernel(sc, n_own, n_par, i0, i1, i2, i3, o0, o1, o2, o3, shift, act, slope, y_own, y_par, wi, wo):
    rows = n_own.shape[0]
    tokens = jnp.concatenate([n_own[...], n_par[...]], axis=0)
    total = jnp.zeros((2 * rows, n_own.shape[1]), f32)
    for s, (i, o) in enumerate(((i0, o0), (i1, o1), (i2, o2), (i3, o3))):
        weights_of(sc, i, wi.at[s])
        weights_of(sc, o, wo.at[s])
        inner = nn(tokens, wi[s]) + shift[s : s + 1, :]
        phi = 0.5 * (1.0 + lax.erf(inner * math.sqrt(0.5)))
        dens = jnp.exp(-0.5 * inner * inner) * (1.0 / math.sqrt(2.0 * math.pi))
        a = (inner * phi).astype(b16)
        act[s] = a
        slope[s] = (phi + inner * dens).astype(slope.dtype)
        total += nn(a, wo[s])
    y_own[...] = total[:rows]
    y_par[...] = total[rows:]


def close_kernel(sc, hat1, y_own, y_par, vec, cot, result, grad_two, low, sums):
    normed = hat1[...] * vec[3:4] + vec[4:5]
    h, r = normalised(normed + y_own[...] + y_par[...] + vec[5:6])
    result[...] = (h * vec[6:7] + vec[7:8]).astype(b16)
    c = cot[...].astype(f32)
    g = norm_back(c * vec[6:7], h, r)
    grad_two[...] = g
    g_low = g.astype(b16)
    low[...] = g_low
    sums[...] = jnp.zeros(sums.shape, f32)
    sums[0:1, :] = row_sum(g_low.astype(f32))
    sums[1:2, :] = row_sum(c * h)
    sums[2:3, :] = row_sum(c)


def feed_back_kernel(sc, g_own, g_par, i0, i1, i2, i3, o0, o1, o2, o3, slope, gi_out, y_own, y_par, gb, wi, wo):
    rows = g_own.shape[0]
    grads = jnp.concatenate([g_own[...], g_par[...]], axis=0)
    total = jnp.zeros((2 * rows, g_own.shape[1]), f32)
    for s, (i, o) in enumerate(((i0, o0), (i1, o1), (i2, o2), (i3, o3))):
        weights_of(sc, i, wi.at[s])
        weights_of(sc, o, wo.at[s])
        gi = (nt(grads, wo[s]) * slope[s].astype(f32)).astype(b16)
        gi_out[s] = gi
        gb[s : s + 1, :] = row_sum(gi.astype(f32))
        total += nt(gi, wi[s])
    y_own[...] = total[:rows]
    y_par[...] = total[rows:]


def feed_grads(sc, s, n_own, n_par, g_own, g_par, act, gi, gb, ranks):
    tokens = jnp.concatenate([n_own[...], n_par[...]], axis=0)
    grads = jnp.concatenate([g_own[...], g_par[...]], axis=0)
    inner = tn(tokens, gi[s])
    outer = tn(act[s], grads)
    half = inner.shape[0] // (2 * ranks)
    piece = outer.shape[0] // ranks
    d = outer.shape[1]
    foot = jnp.concatenate([gb[s : s + 1, :], jnp.zeros((1, d - gb.shape[1]), f32)], axis=1)
    foot = jnp.concatenate([foot, jnp.zeros((7, d), f32)], axis=0)
    ins, outs = [], []
    for k in range(ranks):
        top = inner[2 * k * half : (2 * k + 1) * half]
        ins.append(jnp.concatenate([top, inner[(2 * k + 1) * half : (2 * k + 2) * half]], axis=1))
        outs.append(jnp.concatenate([outer[k * piece : (k + 1) * piece], foot], axis=0))
    return ins, outs


def feed_weights_far_kernel(sc, n_own, n_par, g_own, g_par, act, gi, gb, i_out, o_out):
    ins, outs = feed_grads(sc, 3, n_own, n_par, g_own, g_par, act, gi, gb, i_out.shape[0])
    for k, (i, o) in enumerate(zip(ins, outs)):
        i_out[k] = i.astype(b16)
        o_out[k] = o.astype(b16)


def feed_weights_kernel(sc, n_own, n_par, g_own, g_par, act, gi, gb, i_in, o_in, p0, p1, p2):
    ranks, half = i_in.shape[0], i_in.shape[1]
    for s, out in ((1, p1), (2, p2), (0, p0)):
        ins, outs = feed_grads(sc, s, n_own, n_par, g_own, g_par, act, gi, gb, ranks)
        for k, (i, o) in enumerate(zip(ins, outs)):
            if s == 2:
                i = i + i_in[k].astype(f32)
            if s == 1:
                o = o + o_in[k].astype(f32)
            out[k, :half] = i.astype(b16)
            out[k, half:] = o.astype(b16)


def first_back_kernel(sc, grad_two, y_own, y_par, hat, rate, vec, own, par, grad_one, low, b0, b1, b2, b3, sums, w):
    lay_out(sc, w, own, par)
    gn = grad_two[...] + y_own[...] + y_par[...]
    h = hat[...]
    g = norm_back(gn * vec[3:4], h, rate[:, 0:1])
    grad_one[...] = g
    g_low = g.astype(b16)
    low[...] = g_low
    sums[...] = jnp.zeros(sums.shape, f32)
    sums[0:1, :] = row_sum(g_low.astype(f32))
    sums[1:2, :] = row_sum(gn * h)
    sums[2:3, :] = row_sum(gn)
    half = w.shape[2]
    lo, hi = g_low[:, :half], g_low[:, half:]
    for s, b in enumerate((b0, b1, b2, b3)):
        at = group_rows(sc, s, b.shape[1])
        b[...] = (nt(lo, w[0, at, :]) + nt(hi, w[1, at, :])).astype(b16)


def out_weights_kernel(sc, low, a0, a1, a2, a3, gw_own, gw_par, both):
    c = sc[1]
    ranks, half = gw_own.shape[0], gw_own.shape[1]
    width = low.shape[1] // 2
    lo, hi = low[:, :width], low[:, width:]
    mine = jnp.where(c == 0, lo, hi)
    other = jnp.where(c == 0, hi, lo)
    for s, a in enumerate((a0, a1, a2, a3)):
        at = group_rows(sc, s, a.shape[1])
        both[0, at, :] = tn(a[...], mine).astype(b16)
        both[1, at, :] = tn(a[...], other).astype(b16)
    for k in range(ranks):
        for side in range(2):
            rows = slice((2 * k + side) * half, (2 * k + side + 1) * half)
            gw_own[k, :, side * width : (side + 1) * width] = both[0, rows, :]
            gw_par[k, :, side * width : (side + 1) * width] = both[1, rows, :]


def finish_feed_kernel(sc, near, far, d_inner, d_outer, d_shift, d_out):
    z, c, g = sc[0], sc[1], sc[3]
    half = d_inner.shape[0] // 2
    piece = near.shape[1] - 8 - 2 * half
    ranks = d_inner.shape[1] // (2 * GROUPS * piece)
    width = d_out.shape[1] // 2
    tops, feet = [], []
    for core in range(2):
        total = jnp.zeros((half, 2 * width), f32)
        for k in range(GROUPS):
            at = g ^ k
            block = jnp.where(core == c, near[at], far[at]).astype(f32)
            total += block[half + piece + 8 :]
            row = (core * GROUPS + k) * piece
            d_outer[row : row + piece, :] = block[half : half + piece]
            tops.append(block[:half])
            foot = block[half + piece : half + piece + 1]
            shift = jnp.zeros((1, piece), f32)
            for y in range(ranks):
                shift = jnp.where(z == y, foot[:, y * piece : (y + 1) * piece], shift)
            feet.append(shift)
        for side in range(2):
            at = slice(side * half, (side + 1) * half)
            d_out[at, core * width : (core + 1) * width] = total[:, side * width : (side + 1) * width]
    d_shift[...] = jnp.concatenate(feet, axis=1)
    wide = ranks * piece
    for y in range(ranks):
        for side in range(2):
            low = side * wide + y * piece
            width = 2 * GROUPS * piece
            d_inner[side * half : (side + 1) * half, y * width : (y + 1) * width] = jnp.concatenate(
                [t[:, low : low + piece] for t in tops], axis=1
            )


def finish_kernel(sc, near, far, d_query, d_key, d_value, vec):
    z, c, g = sc[0], sc[1], sc[3]
    dz, d = d_query.shape
    half = dz // 2
    hd = d // HEADS
    per_group = HEADS // GROUPS
    wide = 2 * per_group * hd
    rows = [[None] * GROUPS, [None] * GROUPS]
    total = jnp.zeros((8, d), f32)
    for core in range(2):
        queries, keys, values = [], [], []
        for k in range(GROUPS):
            block = jnp.where(core == c, near[g ^ k], far[g ^ k]).astype(f32)
            for h in range(per_group):
                queries.append(block[:half, 2 * h * hd : (2 * h + 1) * hd] * 0.125)
                keys.append(block[:half, wide + 2 * h * hd : wide + (2 * h + 1) * hd])
                values.append(block[:half, wide + (2 * h + 1) * hd : wide + (2 * h + 2) * hd])
            total += block[half:]
            rows[core][k] = block[half : half + 1]
        at = slice(core * half, (core + 1) * half)
        d_query[at] = jnp.concatenate(queries, axis=1)
        d_key[at] = jnp.concatenate(keys, axis=1)
        d_value[at] = jnp.concatenate(values, axis=1)
    queries, values = [], []
    for k in range(GROUPS):
        row = rows[0][k] + rows[1][k]
        for h in range(per_group):
            queries.append(row[:, 2 * h * hd : (2 * h + 1) * hd] * 0.125)
            values.append(row[:, wide + (2 * h + 1) * hd : wide + (2 * h + 2) * hd])
    full = jnp.concatenate([jnp.concatenate(queries, axis=1), jnp.concatenate(values, axis=1), total[1:7]], axis=0)
    picked = jnp.zeros((8, dz), f32)
    for k in range(d // dz):
        picked = jnp.where(z == k, full[:, k * dz : (k + 1) * dz], picked)
    vec[...] = picked


def per_device(
    tokens,
    segments,
    w_query,
    b_query,
    w_key,
    w_value,
    b_value,
    w_out,
    b_out,
    gain_attention,
    bias_attention,
    w_inner,
    b_inner,
    w_outer,
    b_outer,
    gain_feed,
    bias_feed,
    cotangent,
):
    n = lax.axis_size("ctx")
    ranks = lax.axis_size("fsdp")
    place = lax.axis_index("ctx")
    z = lax.axis_index("fsdp")
    rows, d = tokens.shape[1], tokens.shape[2]
    ff = w_inner.shape[1]
    c, chip = place & 1, place >> 1
    g, r = chip % GROUPS, chip // GROUPS
    sets = n // GROUPS
    rank = r * 2 + c
    per_group = HEADS // GROUPS
    hd = d // HEADS
    gw = per_group * hd
    dz, fz = d // ranks, ff // ranks
    half = dz // 2
    piece = fz // (2 * GROUPS)
    cols = ranks * piece
    wide = per_group * 2 * hd
    sc = jnp.stack([z, c, rank, g]).astype(jnp.int32)
    X, Y, CORE = 2, 4, 1
    flips = [(t & 1) | ((t >> 1) * 2 * GROUPS) for t in range(sets)]

    def over_z(x):
        return [x] + [swap(x, "fsdp", a) for a in range(1, ranks)]

    def over_group(x):
        return [x] + [swap(x, "ctx", s << 1) for s in range(1, GROUPS)]

    def spread(kernel, operands, size, name):
        return whole_call(
            kernel,
            [shape(size, f32)] + [shape(size, b16)] * (ranks - 1),
            1 + len(operands),
            name=name,
        )(sc, *operands)

    tok = tokens[0]
    toks = over_group(tok)

    vectors = (b_query, b_value, b_out, gain_attention, bias_attention, b_outer, gain_feed, bias_feed, b_inner)
    (first,) = whole_call(
        pack_first_kernel, [shape((half + 8, d), b16)], 13, name="pack_first"
    )(sc, w_query, w_key, w_value, *vectors)
    got1, got2 = swap(first, "fsdp", 1), swap(first, "fsdp", 2)
    first_all = jnp.stack([first, got1, got2] + [swap(after(first, got1), "fsdp", a) for a in range(3, ranks)])
    proj_own = first_all[:, :half]
    proj_par = swap(proj_own, "ctx", CORE)
    vec, shift_qkv, shift_inner = whole_call(
        vectors_kernel,
        [shape((8, d), f32), shape((1, 2 * wide), f32), shape((GROUPS, cols), f32)],
        2,
        [pltpu.VMEM((8, d), f32), pltpu.VMEM((2 * GROUPS, cols), f32)],
        name="vectors",
    )(sc, first_all[:, half:])

    q, kv, w_qkv = whole_call(
        project_kernel,
        [shape((GROUPS, rows, wide), b16), shape((GROUPS, rows, wide), b16), shape((d, 2 * wide), b16)],
        8,
        name="project",
    )(sc, *toks, proj_own, proj_par, shift_qkv)
    wi, second = whole_call(
        pack_feed_kernel, [shape((dz, cols), b16), shape((piece + half, d), b16)], 4, name="pack_feed"
    )(sc, after(w_inner, first), w_outer, w_out)
    wi_parts = over_z(after(wi, got2))
    kvs = [kv] + [swap(after(kv, *wi_parts), "ctx", f) for f in flips[1:]]
    wo_parts = over_z(after(second, q))

    seg = segments[0].reshape(n, rows)
    begin, end = seg[:, 0], seg[:, -1]
    span = jnp.stack(
        [
            jnp.sum((end[None, :] < begin[:, None]).astype(jnp.int32), axis=1),
            jnp.sum((begin[None, :] <= end[:, None]).astype(jnp.int32), axis=1),
        ],
        axis=1,
    )
    seg_rows = seg.reshape(n, 1, rows)
    seg_cols = jnp.broadcast_to(seg[:, :, None], (n, rows, 128))

    smem = pl.BlockSpec(memory_space=pltpu.SMEM)

    def fixed(dims):
        return pl.BlockSpec(dims, lambda s: (0,) * len(dims))

    def stepped(dims):
        return pl.BlockSpec((1,) + dims, lambda s: (s,) + (0,) * len(dims))

    kv_specs = [fixed((GROUPS, rows, wide))] * sets

    def attend(q, start, count):
        def falling(dims):
            return pl.BlockSpec((1,) + dims, lambda s: (start - s,) + (0,) * len(dims))

        return pl.pallas_call(
            functools.partial(attend_kernel, start),
            grid=(count,),
            in_specs=[smem, smem, falling((rows, wide)), fixed((n, 1, rows)), fixed((n, rows, 128))] + kv_specs,
            out_specs=[stepped((rows, gw)), stepped((rows, gw)), stepped((8, rows))],
            out_shape=[shape((count, rows, gw), f32), shape((count, rows, gw), b16), shape((count, 8, rows), f32)],
            scratch_shapes=[
                pltpu.VMEM((n, rows, wide), b16),
                pltpu.VMEM((per_group, n, rows, rows), f32),
                pltpu.VMEM((per_group, rows, 128), f32),
                pltpu.VMEM((per_group, rows, 128), f32),
            ],
            name="attend",
            cost_estimate=cost("attend"),
        )(sc, span, q, seg_rows, seg_cols, *kvs)

    wi_z = jnp.stack(wi_parts)
    wi1, wi2 = swap(wi_z, "ctx", X), swap(after(wi_z, *kvs), "ctx", Y)
    seg_rows = after(seg_rows, wi_z)
    mixed_far, low_far, logs_far = attend(q, GROUPS - 1, 2)
    wi3 = swap(after(wi1, low_far, wi2), "ctx", Y)
    mixed_near, low_near, logs_near = attend(after(q, low_far), 1, 2)
    wo_parts = after(tuple(wo_parts), low_near, wi3)
    wo_z, wout_own = whole_call(
        split_second_kernel,
        [shape((ranks, piece, d), b16), shape((ranks, half, d), b16)],
        1 + ranks,
        name="split_second",
    )(sc, *wo_parts)
    wo1, wo2 = swap(wo_z, "ctx", X), swap(wo_z, "ctx", Y)
    wo3 = swap(wo2, "ctx", X)
    atts = [low_near[1], swap(low_near[0], "ctx", X), swap(low_far[1], "ctx", Y), swap(low_far[0], "ctx", X + Y)]
    wout_par = swap(after(wout_own, atts[3]), "ctx", CORE)
    wis, wos = (wi_z, wi1, wi2, wi3), (wo_z, wo1, wo2, wo3)

    hat1, rate1, low = whole_call(
        out_kernel,
        [shape((rows, d), f32), shape((rows, 128), f32), shape((rows, d), b16)],
        9,
        [pltpu.VMEM((2, d, d // 2), b16)],
        name="out",
    )(sc, tok, *atts, wout_own, wout_par, vec)
    low_par = swap(low, "ctx", CORE)

    scratch = [pltpu.VMEM((GROUPS, d, cols), b16), pltpu.VMEM((GROUPS, cols, d), b16)]
    hidden = (GROUPS, 2 * rows, cols)
    act, slope, y_own, y_send = whole_call(
        feed_kernel,
        [shape(hidden, b16), shape(hidden, b16), shape((rows, d), f32), shape((rows, d), f32)],
        12,
        scratch,
        name="feed",
    )(sc, low, low_par, *wis, *wos, shift_inner)
    y_par = swap(y_send, "ctx", CORE)

    result, grad_two, gol, sums_two = whole_call(
        close_kernel,
        [shape((rows, d), b16), shape((rows, d), f32), shape((rows, d), b16), shape((8, d), f32)],
        6,
        name="close",
    )(sc, hat1, y_own, y_par, vec, cotangent[0])
    gol_par = swap(gol, "ctx", CORE)

    gi, gn_own, gn_send, gb_inner = whole_call(
        feed_back_kernel,
        [shape(hidden, b16), shape((rows, d), f32), shape((rows, d), f32), shape((GROUPS, cols), f32)],
        12,
        scratch,
        name="feed_back",
    )(sc, gol, gol_par, *wis, *wos, slope)
    gn_par = swap(gn_send, "ctx", CORE)

    grad_one, gbl, *ga, sums_one = whole_call(
        first_back_kernel,
        [shape((rows, d), f32), shape((rows, d), b16)] + [shape((rows, gw), b16)] * GROUPS + [shape((8, d), f32)],
        9,
        [pltpu.VMEM((2, d, d // 2), b16)],
        name="first_back",
    )(sc, grad_two, gn_own, gn_par, hat1, rate1, vec, wout_own, wout_par)
    grads_att = [ga[0]] + [swap(ga[s], "ctx", s << 1) for s in range(1, GROUPS)]

    far_i, far_o = whole_call(
        feed_weights_far_kernel,
        [shape((ranks, half, d), b16), shape((ranks, piece + 8, d), b16)],
        8,
        name="feed_weights_far",
    )(sc, low, low_par, gol, gol_par, act, gi, after(gb_inner, gbl))
    in_i, in_o = swap(far_i, "ctx", X), swap(far_o, "ctx", Y)

    gwout_own, gwout_send = whole_call(
        out_weights_kernel,
        [shape((ranks, half, d), b16)] * 2,
        6,
        [pltpu.VMEM((2, d, d // 2), b16)],
        name="out_weights",
    )(sc, gbl, *atts)
    out_own, *out_sends = spread(
        spread_out_kernel, (gwout_own, swap(gwout_send, "ctx", CORE)), (half, d), "spread_out"
    )
    out_got = [swap(send, "fsdp", a + 1) for a, send in enumerate(out_sends)]

    def attend_back(start, count, grads, mixed, logs, before, ends):
        def falling(dims):
            return pl.BlockSpec((1,) + dims, lambda s: (start - s,) + (0,) * len(dims))

        begins = not before
        whole_kv = [shape((GROUPS, rows, wide), f32)] + [shape((GROUPS, rows, wide), b16)] * (sets - 1)
        return pl.pallas_call(
            functools.partial(attend_back_kernel, (start, count, begins, ends)),
            grid=(count,),
            in_specs=[smem, smem, falling((rows, wide)), fixed((n, 1, rows)), fixed((n, rows, 128))]
            + [fixed((rows, gw))] * count
            + [stepped((rows, gw)), stepped((8, rows))]
            + kv_specs
            + [fixed((n, rows, wide))] * len(before),
            out_specs=[stepped((rows, wide))] + (kv_specs if ends else [fixed((n, rows, wide))]),
            out_shape=[shape((count, rows, wide), b16)] + (whole_kv if ends else [shape((n, rows, wide), f32)]),
            scratch_shapes=[
                pltpu.VMEM((n, rows, wide), b16),
                pltpu.VMEM((n, rows, wide), f32),
                pltpu.VMEM((per_group, rows, 128), f32),
                pltpu.VMEM((per_group, 2 * rows, 128), b16),
            ],
            name="attend_back",
            cost_estimate=cost("attend_back"),
        )(sc, span, q, seg_rows, seg_cols, *grads, mixed, logs, *kvs, *before)

    dq_far, dkv_part = attend_back(GROUPS - 1, 2, (grads_att[3], after(grads_att[2], grads_att[1])), mixed_far, logs_far, (), False)
    packs = whole_call(
        feed_weights_kernel,
        [shape((ranks, half + piece + 8, d), b16)] * 3,
        10,
        name="feed_weights",
    )(sc, low, low_par, gol, gol_par, act, gi, after(gb_inner, dq_far, *out_got), in_i, in_o)
    pack0, pack1, pack2 = packs
    pack1, pack2 = swap(pack1, "ctx", X), swap(pack2, "ctx", Y)

    dq_near, dkv_own, *dkv_send = attend_back(
        1, 2, (grads_att[1], grads_att[0]), mixed_near, after(logs_near, pack0), (dkv_part,), True
    )
    dkv_send = list(after(tuple(dkv_send), pack1, pack2))
    pack0, pack1, pack2, out_got = after((pack0, pack1, pack2, tuple(out_got)), dq_near)
    feed_own, *feed_sends = spread(
        spread_feed_kernel, (pack0, pack1, pack2), (half + piece + 8, d), "spread_feed"
    )
    feed_got = [swap(send, "fsdp", a + 1) for a, send in enumerate(feed_sends)]
    dkv_in = swap(dkv_send[0], "ctx", flips[1])
    for t in range(2, sets):
        dkv_own = dkv_own + swap(dkv_send[t - 1], "ctx", flips[t]).astype(f32)

    def all_sum(x):
        total = x
        for t in range(1, sets // 2):
            total = total + swap(x, "ctx", t * 2 * GROUPS)
        return total

    keep, give, sums, grads_qkv = whole_call(
        project_weights_kernel,
        [
            shape((ranks, half, 2 * wide), f32),
            shape((ranks, half, 2 * wide), b16),
            shape((8, d), f32),
            shape((GROUPS, rows, 2 * wide), b16),
        ],
        11,
        [pltpu.VMEM((d, 2 * wide), f32)],
        name="project_weights",
    )(sc, *toks, dq_far, dq_near, dkv_own, dkv_in, sums_one, sums_two)
    got = swap(give, "ctx", CORE)

    qkv_own, *qkv_sends = spread(spread_kernel, (keep, got, sums), (half + 8, 2 * wide), "spread")
    qkv_got = [swap(send, "fsdp", a + 1) for a, send in enumerate(qkv_sends)]

    dx_own, *dxs = whole_call(
        project_back_kernel,
        [shape((rows, d), f32)] + [shape((rows, d), b16)] * (GROUPS - 1),
        4,
        name="project_back",
    )(sc, grads_qkv, w_qkv, after(grad_one, qkv_own))
    grad_input = dx_own
    for s in range(1, GROUPS):
        grad_input = grad_input + swap(dxs[s - 1], "ctx", s << 1).astype(f32)

    def total_of(own, got):
        total = own
        for part in got:
            total = total + part.astype(f32)
        return all_sum(total).astype(b16)

    def everywhere(x):
        pieces = jnp.stack(over_group(x))
        return pieces, swap(pieces, "ctx", CORE)

    feed_got = after(tuple(feed_got), qkv_own)
    feed_near, feed_far = everywhere(
        jnp.concatenate([total_of(feed_own, feed_got), total_of(out_own, out_got)], axis=0)
    )
    d_inner, d_outer, d_shift, d_out = whole_call(
        finish_feed_kernel,
        [shape((dz, ff), f32), shape((fz, d), f32), shape((1, fz), f32), shape((dz, d), f32)],
        3,
        name="finish_feed",
    )(sc, feed_near, feed_far)
    d_query, d_key, d_value, vs = whole_call(
        finish_kernel,
        [shape((dz, d), f32)] * 3 + [shape((8, dz), f32)],
        3,
        name="finish",
    )(sc, *everywhere(total_of(qkv_own, qkv_got)))

    return (
        result[None],
        grad_input[None],
        d_query,
        vs[0],
        d_key,
        d_value,
        vs[1],
        d_out,
        vs[2],
        vs[3],
        vs[4],
        d_inner,
        d_shift[0],
        d_outer,
        vs[5],
        vs[6],
        vs[7],
    )


def solution(mesh):
    rows = P("fsdp", "ctx", None)
    matrix = P("fsdp", None)
    vector = P("fsdp")
    return jax.shard_map(
        per_device,
        mesh=mesh,
        in_specs=(rows, matrix, matrix, vector, matrix, matrix, vector, matrix, vector, vector, vector)
        + (matrix, vector, matrix, vector, vector, vector, rows),
        out_specs=(rows, rows, matrix, vector, matrix, matrix, vector, matrix, vector, vector, vector)
        + (matrix, vector, matrix, vector, vector, vector),
        check_vma=False,
    )
```
